32 devices in a mesh: expert: 8 (over z, x), dp: 4 (over y, core).
Axes of the slice: x: 2, y: 2, z: 4, core: 2. Of those that a mesh axis runs over, the one named last changes fastest.
Arguments:
- enc_state: bfloat16 [4, 8, 256, 1024], P('dp', 'expert'), may hold values from -6 to 6
- baseline: bfloat16 [4, 8, 256, 1024], P('dp', 'expert'), may hold values from -6 to 6
- enc_keys: bfloat16 [4, 8, 256, 1024], P('dp', 'expert'), may hold values from -4 to 4
- dec_queries: bfloat16 [4, 8, 128, 1024], P('dp', 'expert'), may hold values from -200 to 200
- out_mult: bfloat16 [4, 8, 128, 1024], P('dp', 'expert'), may hold values from -6 to 6
- doc_lengths: int32 [4, 8], P('dp', 'expert'), may hold values from 128 to 256, as said below
- expert_ids: int32 [4, 8, 256], P('dp', 'expert'), may hold values from 0 to 15
- slot_ids: int32 [4, 8, 256], P('dp', 'expert'), may hold values from 0 to 31, as said below
- gate_prob: float32 [4, 8, 256], P('dp', 'expert'), may hold values from 0.2 to 1
- norm_gain: float32 [1024], replicated, may hold values from 0.5 to 2
- w_in: bfloat16 [16, 1024, 2816], P('expert', None, 'dp'), may hold values from -0.1875 to 0.1875
- w_out_t: bfloat16 [16, 1024, 2816], P('expert', None, 'dp'), may hold values from -0.109375 to 0.109375
- w_value: bfloat16 [1024, 1024], replicated, may hold values from -0.1875 to 0.1875
Outputs:
- enc_mult: bfloat16 [4, 8, 256, 1024], P('dp', 'expert')
The draws below stay inside these ranges and needn't reach their ends.
Inputs may be any that keep to these rules, and one draw needn't show every extreme that they name: `slot_ids`: within one document no two tokens share an expert and a slot, and every token has a slot; one expert has all 32 slots used in every document. `doc_lengths`: some document has all 256 tokens.
All inputs are finite; a program needn't handle non-finite values.
Results may differ from the reference program's by a relative error of at most 0.0069.
Values may be sent and summed in bfloat16 or wider, within the bound.
A program may use at most 128 MiB of HBM per device.

```python
import math
import jax
import jax.numpy as jnp
from jax import lax

D = 1024
FF = 2816
HEADS = 16
HEAD_DIM = 64
ENC_LEN = 256
DEC_LEN = 128
EXPERTS = 16
CAP = 32
GROUPS = 4
DOC_GRP = 8


def routing_draw(key):
    levels = jax.random.randint(jax.random.fold_in(key, 101), (EXPERTS,), 0, 4)
    busiest = jax.random.randint(jax.random.fold_in(key, 102), (), 0, EXPERTS)
    levels = jnp.where(jnp.arange(EXPERTS) == busiest, 9, levels)
    jitter = jax.random.randint(jax.random.fold_in(key, 103), (GROUPS, DOC_GRP, EXPERTS, CAP), 0, 3072)
    scores = (levels[:, None] * 1024 + jitter).reshape(GROUPS, DOC_GRP, EXPERTS * CAP)
    ranked = jnp.argsort(-scores, axis=-1, stable=True)[:, :, :ENC_LEN]
    shuffle_keys = jax.random.randint(jax.random.fold_in(key, 104), (GROUPS, DOC_GRP, ENC_LEN), 0, 2 ** 30)
    shuffle = jnp.argsort(shuffle_keys, axis=-1, stable=True)
    chosen = jnp.take_along_axis(ranked, shuffle, axis=-1)
    return ((chosen // CAP).astype(jnp.int32), (chosen % CAP).astype(jnp.int32))


def attention_draw(key):
    keys = jnp.clip(jax.random.normal(jax.random.fold_in(key, 201), (GROUPS, DOC_GRP, ENC_LEN, D), jnp.float32), -4.0, 4.0)
    queries = 0.5 * jnp.clip(jax.random.normal(jax.random.fold_in(key, 202), (GROUPS, DOC_GRP, DEC_LEN, D), jnp.float32), -6.0, 6.0)
    return (keys, queries)


def draw_enc_keys(key, part):
    return attention_draw(key)[0].astype(jnp.bfloat16)


def draw_dec_queries(key, part):
    return attention_draw(key)[1].astype(jnp.bfloat16)


def draw_doc_lengths(key, part):
    doc_len = jax.random.randint(jax.random.fold_in(key, 301), (GROUPS, DOC_GRP), ENC_LEN // 2, ENC_LEN + 1)
    full_doc = jax.random.randint(jax.random.fold_in(key, 302), (), 0, GROUPS * DOC_GRP)
    doc_index = jnp.arange(GROUPS * DOC_GRP).reshape(GROUPS, DOC_GRP)
    return jnp.where(doc_index == full_doc, ENC_LEN, doc_len).astype(jnp.int32)


def draw_expert_ids(key, part):
    return routing_draw(key)[0]


def draw_slot_ids(key, part):
    return routing_draw(key)[1]


def block_scale(stream_key, dims, shards, least, top_value):
    loudness, own = 1.0, jax.random.fold_in(stream_key, 6)
    for axis_at, shards_of in shards:
        heights = jnp.exp(jax.random.uniform(jax.random.fold_in(own, axis_at), (shards_of,), jnp.float32, least / len(shards), top_value / len(shards)))
        loudness = loudness * jnp.repeat(heights, dims[axis_at] // shards_of).reshape([-1 if axis == axis_at else 1 for axis in range(len(dims))])
    return loudness


def normal_values(own_key, shape, deviation, reach, cuts=(), held_as=jnp.bfloat16):
    factor_of = block_scale(own_key, shape, cuts, -0.22, 0.18) if cuts else 1.0
    values = jax.random.normal(own_key, shape, jnp.float32) * deviation * factor_of
    return jnp.minimum(jnp.maximum(values, -reach), reach).astype(held_as)


def setup_inputs(seed: int = 0) -> dict:
    streams_of = jax.random.split(jax.random.key(seed), 14)
    return {
        "enc_state": normal_values(streams_of[0], (GROUPS, DOC_GRP, ENC_LEN, D), 1.0, 6.0, ((0, 4), (1, 8))),
        "baseline": normal_values(streams_of[1], (GROUPS, DOC_GRP, ENC_LEN, D), 1.0, 6.0, ((0, 4), (1, 8))),
        "enc_keys": draw_enc_keys(jax.random.fold_in(streams_of[13], 71), 0),
        "dec_queries": draw_dec_queries(jax.random.fold_in(streams_of[13], 71), 0),
        "out_mult": normal_values(streams_of[4], (GROUPS, DOC_GRP, DEC_LEN, D), 1.0, 6.0, ((0, 4), (1, 8))),
        "doc_lengths": draw_doc_lengths(jax.random.fold_in(streams_of[13], 71), 0),
        "expert_ids": draw_expert_ids(jax.random.fold_in(streams_of[13], 71), 0),
        "slot_ids": draw_slot_ids(jax.random.fold_in(streams_of[13], 71), 0),
        "gate_prob": jnp.clip(jnp.exp(math.log(1.0) - 1.609438 * jax.random.uniform(streams_of[8], (GROUPS, DOC_GRP, ENC_LEN), jnp.float32) ** block_scale(streams_of[8], (GROUPS, DOC_GRP, ENC_LEN), ((0, 4), (1, 8)), -0.2, 0.2)), 0.2, 1.0),
        "norm_gain": jnp.clip(jnp.exp(jax.random.uniform(streams_of[9], (D,), jnp.float32, math.log(0.5), math.log(2.0))), 0.5, 2.0),
        "w_in": normal_values(streams_of[10], (EXPERTS, D, FF), D ** -0.5, 0.1875, ((0, 8), (2, 4))),
        "w_out_t": normal_values(streams_of[11], (EXPERTS, D, FF), FF ** -0.5, 0.109375, ((0, 8), (2, 4))),
        "w_value": normal_values(streams_of[12], (D, D), D ** -0.5, 0.1875),
    }


def rescale(pre_act, base_act):
    upper_part = jnp.maximum(jnp.maximum(pre_act, base_act), 0.0)
    lower_part = jnp.maximum(-jnp.minimum(pre_act, base_act), 0.0)
    return upper_part / (upper_part + lower_part + jnp.where(upper_part > 0.0, 0.0, 1.0))

def attend(query_rows, key_rows, mult_rows, length, w_value):
    enc_len = key_rows.shape[0]
    dec_len = query_rows.shape[0]
    queries = query_rows.astype(jnp.float32).reshape(dec_len, HEADS, HEAD_DIM)
    keys = key_rows.astype(jnp.float32).reshape(enc_len, HEADS, HEAD_DIM)
    mults = mult_rows.astype(jnp.float32).reshape(dec_len, HEADS, HEAD_DIM)
    scores = jnp.einsum('qhd,khd->hqk', queries, keys) * (1.0 / math.sqrt(HEAD_DIM))
    valid = jnp.arange(enc_len, dtype=jnp.int32) < length
    scores = jnp.where(valid[None, None, :], scores, -jnp.inf)
    top_score = lax.optimization_barrier(jnp.max(scores, axis=-1, keepdims=True))
    expo = jnp.exp(scores - top_score)
    attn = (expo / lax.optimization_barrier(jnp.sum(expo, axis=-1, keepdims=True))).astype(jnp.bfloat16)
    value_mult = jnp.einsum('hqk,qhd->khd', attn.astype(jnp.float32), mults).astype(jnp.bfloat16)
    return jnp.dot(value_mult.reshape(enc_len, HEADS * HEAD_DIM), w_value.T, preferred_element_type=jnp.float32)

def reference(enc_state, baseline, enc_keys, dec_queries, out_mult, doc_lengths, expert_ids, slot_ids, gate_prob, norm_gain, w_in, w_out_t, w_value):
    n_docs = GROUPS * DOC_GRP
    flat_queries = dec_queries.reshape(n_docs, DEC_LEN, D)
    flat_keys = enc_keys.reshape(n_docs, ENC_LEN, D)
    flat_mults = out_mult.reshape(n_docs, DEC_LEN, D)
    flat_len = doc_lengths.reshape(n_docs)
    layer_mult = lax.map(lambda item: attend(item[0], item[1], item[2], item[3], w_value), (flat_queries, flat_keys, flat_mults, flat_len))
    tokens = enc_state.reshape(n_docs, ENC_LEN, D).astype(jnp.float32)
    row_scale = norm_gain.astype(jnp.float32) * lax.rsqrt(lax.optimization_barrier(jnp.mean(tokens * tokens, axis=-1, keepdims=True)) + 1e-06)
    inputs = (tokens * row_scale).astype(jnp.bfloat16)
    base_inputs = (baseline.reshape(n_docs, ENC_LEN, D).astype(jnp.float32) * row_scale).astype(jnp.bfloat16)
    scaled_mult = (gate_prob.reshape(n_docs, ENC_LEN, 1).astype(jnp.float32) * layer_mult).astype(jnp.bfloat16)
    doc_index = jnp.broadcast_to(jnp.arange(n_docs, dtype=jnp.int32)[:, None], (n_docs, ENC_LEN))
    flat_ids = expert_ids.reshape(n_docs, ENC_LEN).astype(jnp.int32)
    flat_slots = slot_ids.reshape(n_docs, ENC_LEN).astype(jnp.int32)

    def place_rows(values):
        filled = jnp.zeros((n_docs, EXPERTS, CAP, D), jnp.bfloat16).at[doc_index, flat_ids, flat_slots].set(values)
        return jnp.swapaxes(filled, 0, 1)
    buf_in = place_rows(inputs)
    buf_base = place_rows(base_inputs)
    buf_mult = place_rows(scaled_mult)

    def one_expert(item):
        weight_in, weight_out, rows_in, rows_base, rows_mult = item
        rows_in = rows_in.reshape(n_docs * CAP, D)
        rows_base = rows_base.reshape(n_docs * CAP, D)
        rows_mult = rows_mult.reshape(n_docs * CAP, D)
        pre_act = jnp.dot(rows_in, weight_in, preferred_element_type=jnp.float32)
        base_act = jnp.dot(rows_base, weight_in, preferred_element_type=jnp.float32)
        hidden_mult = jnp.dot(rows_mult, weight_out, preferred_element_type=jnp.float32)
        act_mult = (rescale(pre_act, base_act) * hidden_mult).astype(jnp.bfloat16)
        slot_mult = jnp.dot(act_mult, weight_in.T, preferred_element_type=jnp.float32).astype(jnp.bfloat16)
        return slot_mult.reshape(n_docs, CAP, D)
    expert_out = lax.map(one_expert, (w_in, w_out_t, buf_in, buf_base, buf_mult))
    per_token = expert_out[flat_ids, doc_index, flat_slots].astype(jnp.float32)
    result = (layer_mult + row_scale * per_token).astype(jnp.bfloat16)
    return result.reshape(GROUPS, DOC_GRP, ENC_LEN, D)
```

```python
import math

import jax
import jax.numpy as jnp
from jax import lax
from jax.sharding import PartitionSpec as P

HEADS = 16
HEAD_DIM = 64


def rescale(pre_act, base_act):
    upper_part = jnp.maximum(jnp.maximum(pre_act, base_act), 0.0)
    lower_part = jnp.maximum(-jnp.minimum(pre_act, base_act), 0.0)
    return upper_part / (upper_part + lower_part + jnp.where(upper_part > 0.0, 0.0, 1.0))


def attend(query_rows, key_rows, mult_rows, length, w_value):
    enc_len = key_rows.shape[0]
    dec_len = query_rows.shape[0]
    queries = query_rows.reshape(dec_len, HEADS, HEAD_DIM)
    keys = key_rows.reshape(enc_len, HEADS, HEAD_DIM)
    mults = mult_rows.reshape(dec_len, HEADS, HEAD_DIM)
    scores = jnp.einsum("qhd,khd->hqk", queries, keys, preferred_element_type=jnp.float32) * (
        1.0 / math.sqrt(HEAD_DIM)
    )
    valid = jnp.arange(enc_len, dtype=jnp.int32) < length
    scores = jnp.where(valid[None, None, :], scores, -jnp.inf)
    top_score = jnp.max(scores, axis=-1, keepdims=True)
    expo = jnp.exp(scores - top_score)
    attn = (expo / jnp.sum(expo, axis=-1, keepdims=True)).astype(jnp.bfloat16)
    value_mult = jnp.einsum("hqk,qhd->khd", attn, mults, preferred_element_type=jnp.float32).astype(
        jnp.bfloat16
    )
    return lax.dot_general(
        value_mult.reshape(enc_len, HEADS * HEAD_DIM),
        w_value,
        (((1,), (1,)), ((), ())),
        preferred_element_type=jnp.float32,
    )


def expert_terms(rows_in, rows_base, rows_mult, part_in, part_out):
    pre_act = jnp.einsum("erd,edf->erf", rows_in, part_in, preferred_element_type=jnp.float32)
    base_act = jnp.einsum("erd,edf->erf", rows_base, part_in, preferred_element_type=jnp.float32)
    hidden_mult = jnp.einsum(
        "erd,edf->erf", rows_mult, part_out, preferred_element_type=jnp.float32
    )
    act_mult = (rescale(pre_act, base_act) * hidden_mult).astype(jnp.bfloat16)
    return jnp.einsum("erf,edf->erd", act_mult, part_in, preferred_element_type=jnp.float32)


def body(
    enc_state,
    baseline,
    enc_keys,
    dec_queries,
    out_mult,
    doc_lengths,
    expert_ids,
    slot_ids,
    gate_prob,
    norm_gain,
    w_in,
    w_out_t,
    w_value,
):
    enc_len = enc_state.shape[2]
    feature_width = enc_state.shape[3]
    local_experts = w_in.shape[0]
    n_experts = local_experts * lax.axis_size("expert")
    n_dp = lax.axis_size("dp")
    near = 2 if n_dp % 2 == 0 else 1
    capacity = max(2, 2 * enc_len // n_experts)

    shards = [(w_in, w_out_t)]
    if near == 2:
        swap = [(i, i ^ 1) for i in range(n_dp)]
        shards.append((lax.ppermute(w_in, "dp", swap), lax.ppermute(w_out_t, "dp", swap)))

    tokens = enc_state[0, 0].astype(jnp.float32)
    row_scale = norm_gain * lax.rsqrt(jnp.mean(tokens * tokens, axis=-1, keepdims=True) + 1e-06)
    inputs = (tokens * row_scale).astype(jnp.bfloat16)
    base_inputs = (baseline[0, 0].astype(jnp.float32) * row_scale).astype(jnp.bfloat16)
    flat_slot = expert_ids[0, 0] * capacity + slot_ids[0, 0]
    onehot = (
        flat_slot[None, :] == jnp.arange(n_experts * capacity, dtype=jnp.int32)[:, None]
    ).astype(jnp.bfloat16)

    def dispatch(values):
        placed = jnp.dot(onehot, values, preferred_element_type=jnp.float32).astype(jnp.bfloat16)
        placed = placed.reshape(n_experts, capacity, feature_width)
        return lax.all_to_all(placed, "expert", split_axis=0, concat_axis=1, tiled=True)

    sent_in = dispatch(inputs)
    sent_base = dispatch(base_inputs)
    layer_mult = attend(
        dec_queries[0, 0], enc_keys[0, 0], out_mult[0, 0], doc_lengths[0, 0], w_value
    )
    scaled_mult = (gate_prob[0, 0][:, None] * layer_mult).astype(jnp.bfloat16)
    sent_mult = dispatch(scaled_mult)
    own_rows = (sent_in, sent_base, sent_mult)

    def partial_sum(rows):
        total = expert_terms(*rows, *shards[0])
        for part in shards[1:]:
            total = total + expert_terms(*rows, *part)
        return total

    far = n_dp // near
    far_rows = []
    for hop in range(1, far):
        ahead = [(i, (i + hop * near) % n_dp) for i in range(n_dp)]
        far_rows.append(tuple(lax.ppermute(a, "dp", ahead) for a in own_rows))
    slot_mult = partial_sum(own_rows)
    for hop in range(1, far):
        back = [((i + hop * near) % n_dp, i) for i in range(n_dp)]
        far_part = partial_sum(far_rows[hop - 1]).astype(jnp.bfloat16)
        slot_mult = slot_mult + lax.ppermute(far_part, "dp", back).astype(jnp.float32)

    returned = lax.all_to_all(
        slot_mult.astype(jnp.bfloat16), "expert", split_axis=1, concat_axis=0, tiled=True
    )
    per_token = lax.dot_general(
        onehot,
        returned.reshape(n_experts * capacity, feature_width),
        (((0,), (0,)), ((), ())),
        preferred_element_type=jnp.float32,
    )
    result = (layer_mult + row_scale * per_token).astype(jnp.bfloat16)
    return result[None, None]


def solution(mesh):
    in_specs = (
        P("dp", "expert", None, None),
        P("dp", "expert", None, None),
        P("dp", "expert", None, None),
        P("dp", "expert", None, None),
        P("dp", "expert", None, None),
        P("dp", "expert"),
        P("dp", "expert", None),
        P("dp", "expert", None),
        P("dp", "expert", None),
        P(),
        P("expert", None, "dp"),
        P("expert", None, "dp"),
        P(),
    )
    out_specs = P("dp", "expert", None, None)
    return jax.shard_map(body, mesh=mesh, in_specs=in_specs, out_specs=out_specs, check_vma=False)
```

```python
import functools
import math

import jax
import jax.numpy as jnp
from jax import lax
from jax.experimental import pallas as pl
from jax.experimental.pallas import tpu as pltpu
from jax.sharding import PartitionSpec as P

HEADS = 16
HEAD_DIM = 64


def rescale(pre_act, base_act):
    upper_part = jnp.maximum(jnp.maximum(pre_act, base_act), 0.0)
    lower_part = jnp.maximum(-jnp.minimum(pre_act, base_act), 0.0)
    return upper_part / (upper_part + lower_part + jnp.where(upper_part > 0.0, 0.0, 1.0))


def attend(query_rows, key_rows, mult_rows, length, w_value):
    enc_len = key_rows.shape[0]
    dec_len = query_rows.shape[0]
    queries = query_rows.reshape(dec_len, HEADS, HEAD_DIM)
    keys = key_rows.reshape(enc_len, HEADS, HEAD_DIM)
    mults = mult_rows.reshape(dec_len, HEADS, HEAD_DIM)
    scores = jnp.einsum("qhd,khd->hqk", queries, keys, preferred_element_type=jnp.float32) * (
        1.0 / math.sqrt(HEAD_DIM)
    )
    valid = jnp.arange(enc_len, dtype=jnp.int32) < length
    scores = jnp.where(valid[None, None, :], scores, -jnp.inf)
    top_score = jnp.max(scores, axis=-1, keepdims=True)
    expo = jnp.exp(scores - top_score)
    attn = (expo / jnp.sum(expo, axis=-1, keepdims=True)).astype(jnp.bfloat16)
    value_mult = jnp.einsum("hqk,qhd->khd", attn, mults, preferred_element_type=jnp.float32).astype(
        jnp.bfloat16
    )
    return lax.dot_general(
        value_mult.reshape(enc_len, HEADS * HEAD_DIM),
        w_value,
        (((1,), (1,)), ((), ())),
        preferred_element_type=jnp.float32,
    )


def expert_terms(rows_in, rows_base, rows_mult, part_in, part_out):
    pre_act = jnp.einsum("erd,edf->erf", rows_in, part_in, preferred_element_type=jnp.float32)
    base_act = jnp.einsum("erd,edf->erf", rows_base, part_in, preferred_element_type=jnp.float32)
    hidden_mult = jnp.einsum(
        "erd,edf->erf", rows_mult, part_out, preferred_element_type=jnp.float32
    )
    act_mult = (rescale(pre_act, base_act) * hidden_mult).astype(jnp.bfloat16)
    return jnp.einsum("erf,edf->erd", act_mult, part_in, preferred_element_type=jnp.float32)


def expert_kernel(
    n_peers,
    n_dp,
    send_in,
    send_base,
    send_mult,
    w_in,
    w_out,
    back,
    all_in,
    all_out,
    near_rows,
    far_rows,
    ratio,
    near_sum,
    far_sum,
    far_got,
    slot_sum,
    weight_sem,
    swap_send,
    swap_recv,
    row_send,
    row_recv,
    hop_send,
    hop_recv,
    part_send,
    part_recv,
    back_send,
    back_recv,
):
    sends = (send_in, send_base, send_mult)
    n_local = w_in.shape[0]
    cap = send_in.shape[1]
    rows = n_peers * cap
    me = lax.axis_index("expert")
    dp = lax.axis_index("dp")
    pair = dp + 1 - 2 * lax.rem(dp, 2)
    across = lax.rem(dp + 2, n_dp)
    mesh_id = pl.DeviceIdType.MESH

    def peer_at(off):
        return lax.rem(me + off, n_peers)

    def source_at(off):
        return lax.rem(me + n_peers - off, n_peers)

    barrier = pltpu.get_barrier_semaphore()
    for off in range(1, n_peers):
        pl.semaphore_signal(barrier, inc=1, device_id={"expert": peer_at(off)}, device_id_type=mesh_id)
    for other in (pair, across):
        pl.semaphore_signal(barrier, inc=1, device_id={"dp": other}, device_id_type=mesh_id)
    pl.semaphore_wait(barrier, n_peers + 1)

    def row_block(buf, a, l, src):
        return buf.at[a, l, pl.ds(pl.multiple_of(src * cap, cap), cap), :]

    def row_copy(a, l, off):
        peer = peer_at(off)
        return pltpu.make_async_remote_copy(
            src_ref=sends[a].at[peer * n_local + l],
            dst_ref=row_block(near_rows, a, l, me),
            send_sem=row_send.at[a, l, off],
            recv_sem=row_recv.at[a, l, off],
            device_id={"expert": peer},
            device_id_type=mesh_id,
        )

    def own_copy(a, l):
        return pltpu.make_async_copy(
            sends[a].at[me * n_local + l], row_block(near_rows, a, l, me), row_recv.at[a, l, 0]
        )

    def send_rows(a, l):
        for off in range(1, n_peers):
            row_copy(a, l, off).start()
        own_copy(a, l).start()

    def hop_copy(a, l, off):
        src = source_at(off)
        return pltpu.make_async_remote_copy(
            src_ref=row_block(near_rows, a, l, src),
            dst_ref=row_block(far_rows, a, l, src),
            send_sem=hop_send.at[a, l, off],
            recv_sem=hop_recv.at[a, l, off],
            device_id={"dp": across},
            device_id_type=mesh_id,
        )

    def relay(a, l):
        own_copy(a, l).wait()
        hop_copy(a, l, 0).start()
        for off in range(1, n_peers):
            row_copy(a, l, off).wait_recv()
            hop_copy(a, l, off).start()

    def wait_far(a, l):
        for off in range(n_peers):
            hop_copy(a, l, off).wait_recv()

    own_weights = []
    for at, (ref, held) in enumerate(((w_in, all_in), (w_out, all_out))):
        copy = pltpu.make_async_copy(ref, held.at[0], weight_sem.at[at])
        copy.start()
        own_weights.append(copy)
    swaps = []
    for l in range(n_local):
        for a in range(3):
            send_rows(a, l)
        if l == 0:
            for at, (ref, held) in enumerate(((w_in, all_in), (w_out, all_out))):
                swap = pltpu.make_async_remote_copy(
                    src_ref=ref,
                    dst_ref=held.at[1],
                    send_sem=swap_send.at[at],
                    recv_sem=swap_recv.at[at],
                    device_id={"dp": pair},
                    device_id_type=mesh_id,
                )
                swap.start()
                swaps.append(swap)

    def ratio_of(buf, half, l):
        @pl.loop(0, 2)
        def _(shard):
            weight = all_in[shard, l]
            pre = jnp.dot(buf[0, l], weight, preferred_element_type=jnp.float32)
            base = jnp.dot(buf[1, l], weight, preferred_element_type=jnp.float32)
            ratio[half, shard] = rescale(pre, base)

    def sum_of(buf, half, l, total):
        @pl.loop(0, 2)
        def _(shard):
            hidden = jnp.dot(buf[2, l], all_out[shard, l], preferred_element_type=jnp.float32)
            act = (ratio[half, shard] * hidden).astype(jnp.bfloat16)
            part = lax.dot_general(
                act, all_in[shard, l], (((1,), (1,)), ((), ())), preferred_element_type=jnp.float32
            )

            @pl.when(shard == 0)
            def _():
                total[...] = part

            @pl.when(shard != 0)
            def _():
                total[...] += part

    def part_copy(l):
        return pltpu.make_async_remote_copy(
            src_ref=far_sum.at[l],
            dst_ref=far_got.at[l],
            send_sem=part_send.at[l],
            recv_sem=part_recv.at[l],
            device_id={"dp": across},
            device_id_type=mesh_id,
        )

    def back_copy(l, off):
        peer = peer_at(off)
        return pltpu.make_async_remote_copy(
            src_ref=slot_sum.at[l, pl.ds(pl.multiple_of(peer * cap, cap), cap), :],
            dst_ref=back.at[me * n_local + l],
            send_sem=back_send.at[l, off],
            recv_sem=back_recv.at[l, off],
            device_id={"expert": peer},
            device_id_type=mesh_id,
        )

    def own_back(l):
        return pltpu.make_async_copy(
            slot_sum.at[l, pl.ds(pl.multiple_of(me * cap, cap), cap), :],
            back.at[me * n_local + l],
            back_recv.at[l, 0],
        )

    def send_back(l):
        part_copy(l).wait_recv()
        slot_sum[l] = (near_sum[l] + far_got[l].astype(jnp.float32)).astype(jnp.bfloat16)
        for off in range(1, n_peers):
            back_copy(l, off).start()
        own_back(l).start()

    def far_part(l):
        wait_far(0, l)
        wait_far(1, l)
        ratio_of(far_rows, 1, l)
        wait_far(2, l)
        sum_of(far_rows, 1, l, near_sum.at[n_local])
        far_sum[l] = near_sum[n_local].astype(jnp.bfloat16)
        part_copy(l).start()

    relay(0, 0)
    relay(1, 0)
    for copy in own_weights:
        copy.wait()
    for swap in swaps:
        swap.wait_recv()
    ratio_of(near_rows, 0, 0)
    relay(2, 0)
    for l in range(n_local):
        sum_of(near_rows, 0, l, near_sum.at[l])
        if l + 1 < n_local:
            relay(0, l + 1)
        far_part(l)
        if l + 1 < n_local:
            relay(1, l + 1)
            ratio_of(near_rows, 0, l + 1)
            send_back(l)
            relay(2, l + 1)
    send_back(n_local - 1)

    for swap in swaps:
        swap.wait_send()
    for l in range(n_local):
        for a in range(3):
            for off in range(n_peers):
                if off:
                    row_copy(a, l, off).wait_send()
                hop_copy(a, l, off).wait_send()
        part_copy(l).wait_send()
        own_back(l).wait()
        for off in range(1, n_peers):
            back_copy(l, off).wait()


def expert_pass(sent, w_in, w_out_t, n_peers, n_dp):
    n_slots, cap, width = sent[0].shape
    n_local, _, part = w_in.shape
    rows = n_peers * cap
    bf16, f32 = jnp.bfloat16, jnp.float32
    dma = pltpu.SemaphoreType.DMA
    vmem = pl.BlockSpec(memory_space=pltpu.VMEM)
    anyw = pl.BlockSpec(memory_space=pl.ANY)
    return pl.pallas_call(
        functools.partial(expert_kernel, n_peers, n_dp),
        out_shape=jax.ShapeDtypeStruct((n_slots, cap, width), bf16),
        in_specs=[vmem, vmem, vmem, anyw, anyw],
        out_specs=vmem,
        scratch_shapes=[
            pltpu.VMEM((2, n_local, width, part), bf16),
            pltpu.VMEM((2, n_local, width, part), bf16),
            pltpu.VMEM((3, n_local, rows, width), bf16),
            pltpu.VMEM((3, n_local, rows, width), bf16),
            pltpu.VMEM((2, 2, rows, part), f32),
            pltpu.VMEM((n_local + 1, rows, width), f32),
            pltpu.VMEM((n_local, rows, width), bf16),
            pltpu.VMEM((n_local, rows, width), bf16),
            pltpu.VMEM((n_local, rows, width), bf16),
            dma((2,)),
            dma((2,)),
            dma((2,)),
            dma((3, n_local, n_peers)),
            dma((3, n_local, n_peers)),
            dma((3, n_local, n_peers)),
            dma((3, n_local, n_peers)),
            dma((n_local,)),
            dma((n_local,)),
            dma((n_local, n_peers)),
            dma((n_local, n_peers)),
        ],
        compiler_params=pltpu.CompilerParams(
            collective_id=0, has_side_effects=True, vmem_limit_bytes=60 * 1024 * 1024
        ),
        name="expert_pass",
    )(*sent, w_in, w_out_t)


def plain_pass(sent, w_in, w_out_t, n_peers, n_dp):
    near = 2 if n_dp % 2 == 0 else 1
    shards = [(w_in, w_out_t)]
    if near == 2:
        swap = [(i, i ^ 1) for i in range(n_dp)]
        shards.append((lax.ppermute(w_in, "dp", swap), lax.ppermute(w_out_t, "dp", swap)))
    own_rows = tuple(
        lax.all_to_all(a, "expert", split_axis=0, concat_axis=1, tiled=True) for a in sent
    )

    def partial_sum(rows):
        total = expert_terms(*rows, *shards[0])
        for part in shards[1:]:
            total = total + expert_terms(*rows, *part)
        return total

    far = n_dp // near
    far_rows = []
    for hop in range(1, far):
        ahead = [(i, (i + hop * near) % n_dp) for i in range(n_dp)]
        far_rows.append(tuple(lax.ppermute(a, "dp", ahead) for a in own_rows))
    slot_mult = partial_sum(own_rows)
    for hop in range(1, far):
        back = [((i + hop * near) % n_dp, i) for i in range(n_dp)]
        far_part = partial_sum(far_rows[hop - 1]).astype(jnp.bfloat16)
        slot_mult = slot_mult + lax.ppermute(far_part, "dp", back).astype(jnp.float32)

    return lax.all_to_all(
        slot_mult.astype(jnp.bfloat16), "expert", split_axis=1, concat_axis=0, tiled=True
    )


def body(
    enc_state,
    baseline,
    enc_keys,
    dec_queries,
    out_mult,
    doc_lengths,
    expert_ids,
    slot_ids,
    gate_prob,
    norm_gain,
    w_in,
    w_out_t,
    w_value,
):
    enc_len = enc_state.shape[2]
    feature_width = enc_state.shape[3]
    local_experts = w_in.shape[0]
    n_experts = local_experts * lax.axis_size("expert")
    n_dp = lax.axis_size("dp")
    capacity = max(2, 2 * enc_len // n_experts)

    tokens = enc_state[0, 0].astype(jnp.float32)
    row_scale = norm_gain * lax.rsqrt(jnp.mean(tokens * tokens, axis=-1, keepdims=True) + 1e-06)
    inputs = (tokens * row_scale).astype(jnp.bfloat16)
    base_inputs = (baseline[0, 0].astype(jnp.float32) * row_scale).astype(jnp.bfloat16)
    flat_slot = expert_ids[0, 0] * capacity + slot_ids[0, 0]
    onehot = (
        flat_slot[None, :] == jnp.arange(n_experts * capacity, dtype=jnp.int32)[:, None]
    ).astype(jnp.bfloat16)

    def dispatch(values):
        placed = jnp.dot(onehot, values, preferred_element_type=jnp.float32).astype(jnp.bfloat16)
        return placed.reshape(n_experts, capacity, feature_width)

    layer_mult = attend(
        dec_queries[0, 0], enc_keys[0, 0], out_mult[0, 0], doc_lengths[0, 0], w_value
    )
    scaled_mult = (gate_prob[0, 0][:, None] * layer_mult).astype(jnp.bfloat16)
    sent = (dispatch(inputs), dispatch(base_inputs), dispatch(scaled_mult))
    n_peers = lax.axis_size("expert")
    fits = n_dp == 4 and capacity % 16 == 0
    returned = (expert_pass if fits else plain_pass)(sent, w_in, w_out_t, n_peers, n_dp)
    per_token = lax.dot_general(
        onehot,
        returned.reshape(n_experts * capacity, feature_width),
        (((0,), (0,)), ((), ())),
        preferred_element_type=jnp.float32,
    )
    result = (layer_mult + row_scale * per_token).astype(jnp.bfloat16)
    return result[None, None]


def solution(mesh):
    in_specs = (
        P("dp", "expert", None, None),
        P("dp", "expert", None, None),
        P("dp", "expert", None, None),
        P("dp", "expert", None, None),
        P("dp", "expert", None, None),
        P("dp", "expert"),
        P("dp", "expert", None),
        P("dp", "expert", None),
        P("dp", "expert", None),
        P(),
        P("expert", None, "dp"),
        P("expert", None, "dp"),
        P(),
    )
    out_specs = P("dp", "expert", None, None)
    return jax.shard_map(body, mesh=mesh, in_specs=in_specs, out_specs=out_specs, check_vma=False)
```

```python
import functools
import math

import jax
import jax.numpy as jnp
from jax import lax
from jax.experimental import pallas as pl
from jax.experimental.pallas import tpu as pltpu
from jax.sharding import PartitionSpec as P

HEADS = 16
HEAD_DIM = 64


def rescale(pre_act, base_act):
    upper_part = jnp.maximum(jnp.maximum(pre_act, base_act), 0.0)
    lower_part = jnp.maximum(-jnp.minimum(pre_act, base_act), 0.0)
    return upper_part / (upper_part + lower_part + jnp.where(upper_part > 0.0, 0.0, 1.0))


def attend(query_rows, key_rows, mult_rows, length, w_value):
    enc_len = key_rows.shape[0]
    dec_len = query_rows.shape[0]
    queries = query_rows.reshape(dec_len, HEADS, HEAD_DIM)
    keys = key_rows.reshape(enc_len, HEADS, HEAD_DIM)
    mults = mult_rows.reshape(dec_len, HEADS, HEAD_DIM)
    scores = jnp.einsum("qhd,khd->hqk", queries, keys, preferred_element_type=jnp.float32) * (
        1.0 / math.sqrt(HEAD_DIM)
    )
    valid = jnp.arange(enc_len, dtype=jnp.int32) < length
    scores = jnp.where(valid[None, None, :], scores, -jnp.inf)
    top_score = jnp.max(scores, axis=-1, keepdims=True)
    expo = jnp.exp(scores - top_score)
    attn = (expo / jnp.sum(expo, axis=-1, keepdims=True)).astype(jnp.bfloat16)
    value_mult = jnp.einsum("hqk,qhd->khd", attn, mults, preferred_element_type=jnp.float32).astype(
        jnp.bfloat16
    )
    return lax.dot_general(
        value_mult.reshape(enc_len, HEADS * HEAD_DIM),
        w_value,
        (((1,), (1,)), ((), ())),
        preferred_element_type=jnp.float32,
    )


def expert_terms(rows_in, rows_base, rows_mult, part_in, part_out):
    pre_act = jnp.einsum("erd,edf->erf", rows_in, part_in, preferred_element_type=jnp.float32)
    base_act = jnp.einsum("erd,edf->erf", rows_base, part_in, preferred_element_type=jnp.float32)
    hidden_mult = jnp.einsum(
        "erd,edf->erf", rows_mult, part_out, preferred_element_type=jnp.float32
    )
    act_mult = (rescale(pre_act, base_act) * hidden_mult).astype(jnp.bfloat16)
    return jnp.einsum("erf,edf->erd", act_mult, part_in, preferred_element_type=jnp.float32)


def times_t(left, right):
    return lax.dot_general(left, right, (((1,), (1,)), ((), ())), preferred_element_type=jnp.float32)


def whole_kernel(
    n_peers,
    n_dp,
    cap,
    chunk,
    state,
    base_state,
    slot_row,
    slot_col,
    gate,
    gain,
    length,
    keys_at,
    queries_at,
    mults_at,
    value_at,
    w_in,
    w_out,
    out,
    keys,
    queries,
    mults,
    value,
    value_mult,
    layer,
    scale,
    sends,
    all_in,
    all_out,
    near_rows,
    far_rows,
    ratio,
    act,
    near_sum,
    far_sum,
    far_got,
    slot_sum,
    back,
    load_sem,
    weight_sem,
    swap_send,
    swap_recv,
    row_send,
    row_recv,
    hop_send,
    hop_recv,
    part_send,
    part_recv,
    back_send,
    back_recv,
):
    n_local = w_in.shape[0]
    tokens, width = state.shape
    rows = n_peers * cap
    n_chunks = width // chunk
    bf16, f32 = jnp.bfloat16, jnp.float32
    me = lax.axis_index("expert")
    dp = lax.axis_index("dp")
    pair = dp + 1 - 2 * lax.rem(dp, 2)
    across = lax.rem(dp + 2, n_dp)
    mesh_id = pl.DeviceIdType.MESH

    loads = []
    for at, (ref, held) in enumerate(
        ((queries_at, queries), (keys_at, keys), (mults_at, mults), (value_at, value))
    ):
        copy = pltpu.make_async_copy(ref, held, load_sem.at[at])
        copy.start()
        loads.append(copy)
    own_weights = []
    for at, (ref, held) in enumerate(((w_in, all_in), (w_out, all_out))):
        copy = pltpu.make_async_copy(ref, held.at[0], weight_sem.at[at])
        copy.start()
        own_weights.append(copy)

    def peer_at(step):
        peer, bit = 0, 1
        while bit < n_peers:
            digit = lax.rem(me // bit, 2)
            peer = peer + bit * (1 - digit if step & bit else digit)
            bit *= 2
        return peer

    barrier = pltpu.get_barrier_semaphore()
    for step in range(1, n_peers):
        pl.semaphore_signal(barrier, inc=1, device_id={"expert": peer_at(step)}, device_id_type=mesh_id)
    for other in (pair, across):
        pl.semaphore_signal(barrier, inc=1, device_id={"dp": other}, device_id_type=mesh_id)

    def place_rows(a, l, values):
        at = lax.broadcasted_iota(jnp.int32, (rows, tokens), 0) + l * rows
        onehot = jnp.where(at == slot_row[...], 1.0, 0.0).astype(bf16)
        sends[a, l] = jnp.dot(onehot, values, preferred_element_type=f32).astype(bf16)

    def block_of(src):
        return pl.ds(pl.multiple_of(src * cap, cap), cap)

    def row_copy(a, l, step):
        peer = peer_at(step)
        return pltpu.make_async_remote_copy(
            src_ref=sends.at[a, l, block_of(peer), :],
            dst_ref=near_rows.at[a, l, block_of(me), :],
            send_sem=row_send.at[a, l, step],
            recv_sem=row_recv.at[a, l, step],
            device_id={"expert": peer},
            device_id_type=mesh_id,
        )

    def own_copy(a, l):
        return pltpu.make_async_copy(
            sends.at[a, l, block_of(me), :], near_rows.at[a, l, block_of(me), :], row_recv.at[a, l, 0]
        )

    def send_rows(a, l):
        own_copy(a, l).start()
        for step in range(n_peers - 1, 0, -1):
            row_copy(a, l, step).start()

    def hop_copy(a, l, step):
        src = block_of(peer_at(step))
        return pltpu.make_async_remote_copy(
            src_ref=near_rows.at[a, l, src, :],
            dst_ref=far_rows.at[a, l, src, :],
            send_sem=hop_send.at[a, l, step],
            recv_sem=hop_recv.at[a, l, step],
            device_id={"dp": across},
            device_id_type=mesh_id,
        )

    def relay(a, l, steps):
        for step in steps:
            if step == 0:
                own_copy(a, l).wait()
            else:
                row_copy(a, l, step).wait_recv()
            hop_copy(a, l, step).start()

    def wait_far(a, l):
        for step in range(n_peers):
            hop_copy(a, l, step).wait_recv()

    close = range(0, 2)
    distant = range(2, n_peers)

    token_rows = state[...].astype(f32)
    scale[...] = gain[...] * lax.rsqrt(
        jnp.mean(token_rows * token_rows, axis=-1, keepdims=True) + 1e-06
    )
    inputs = (token_rows * scale[...]).astype(bf16)
    place_rows(0, 0, inputs)
    pl.semaphore_wait(barrier, n_peers + 1)
    send_rows(0, 0)
    base_inputs = (base_state[...].astype(f32) * scale[...]).astype(bf16)
    place_rows(1, 0, base_inputs)
    send_rows(1, 0)
    for l in range(1, n_local):
        place_rows(0, l, inputs)
        send_rows(0, l)
        place_rows(1, l, base_inputs)
        send_rows(1, l)

    swaps = []
    for at, (ref, held) in enumerate(((w_in, all_in), (w_out, all_out))):
        swap = pltpu.make_async_remote_copy(
            src_ref=ref,
            dst_ref=held.at[1],
            send_sem=swap_send.at[at],
            recv_sem=swap_recv.at[at],
            device_id={"dp": pair},
            device_id_type=mesh_id,
        )
        swap.start()
        swaps.append(swap)

    for l in range(n_local):
        for a in range(2):
            relay(a, l, close)

    for copy in loads:
        copy.wait()

    @pl.loop(0, width // (2 * HEAD_DIM))
    def _(both):
        cols = pl.ds(pl.multiple_of(both * 2 * HEAD_DIM, 2 * HEAD_DIM), 2 * HEAD_DIM)
        query, key, mult = queries[:, cols], keys[:, cols], mults[:, cols]
        first = lax.broadcasted_iota(jnp.int32, query.shape, 1) < HEAD_DIM
        zero = jnp.zeros_like(query)
        found = []
        for head in range(2):
            mine = jnp.where(first, query, zero) if head == 0 else jnp.where(first, zero, query)
            scores = times_t(key, mine) * (1.0 / math.sqrt(HEAD_DIM))
            at = lax.broadcasted_iota(jnp.int32, scores.shape, 0)
            scores = jnp.where(at < length[...], scores, -jnp.inf)
            expo = jnp.exp(scores - jnp.max(scores, axis=0, keepdims=True))
            attn = (expo / jnp.sum(expo, axis=0, keepdims=True)).astype(bf16)
            found.append(jnp.dot(attn, mult, preferred_element_type=f32))
        left = lax.broadcasted_iota(jnp.int32, found[0].shape, 1) < HEAD_DIM
        value_mult[:, cols] = jnp.where(left, found[0], found[1]).astype(bf16)

    def chunk_of(c):
        return pl.ds(pl.multiple_of(c * chunk, chunk), chunk)

    @pl.loop(0, n_chunks)
    def _(c):
        layer[:, chunk_of(c)] = times_t(value_mult[...], value[chunk_of(c), :])

    scaled = (gate[...] * layer[...]).astype(bf16)
    for l in range(n_local):
        place_rows(2, l, scaled)
        send_rows(2, l)
    for l in range(n_local):
        relay(2, l, close)

    def ratio_of(buf, half, l):
        @pl.loop(0, 2)
        def _(shard):
            weight = all_in[shard, l]
            pre = times_t(buf[0, l], weight)
            base = times_t(buf[1, l], weight)
            ratio[half, l, shard] = rescale(pre, base)

    def acts_of(buf, half, l):
        @pl.loop(0, 2)
        def _(shard):
            hidden = times_t(buf[2, l], all_out[shard, l])
            act[shard] = (ratio[half, l, shard] * hidden).astype(bf16)

    def chunk_sum(l, c):
        cols = chunk_of(c)
        return jnp.dot(act[0], all_in[0, l, :, cols], preferred_element_type=f32) + jnp.dot(
            act[1], all_in[1, l, :, cols], preferred_element_type=f32
        )

    def part_copy(l, c):
        return pltpu.make_async_remote_copy(
            src_ref=far_sum.at[l, :, chunk_of(c)],
            dst_ref=far_got.at[l, :, chunk_of(c)],
            send_sem=part_send.at[l, c],
            recv_sem=part_recv.at[l, c],
            device_id={"dp": across},
            device_id_type=mesh_id,
        )

    def near_part(l):
        acts_of(near_rows, 0, l)

        @pl.loop(0, n_chunks)
        def _(c):
            near_sum[l, :, chunk_of(c)] = chunk_sum(l, c)

    def far_part(l):
        acts_of(far_rows, 1, l)

        @pl.loop(0, n_chunks)
        def _(c):
            far_sum[l, :, chunk_of(c)] = chunk_sum(l, c).astype(bf16)
            part_copy(l, c).start()

    def back_copy(l, c, step):
        peer = peer_at(step)
        return pltpu.make_async_remote_copy(
            src_ref=slot_sum.at[l, block_of(peer), chunk_of(c)],
            dst_ref=back.at[l, block_of(me), chunk_of(c)],
            send_sem=back_send.at[l, c, step],
            recv_sem=back_recv.at[l, c, step],
            device_id={"expert": peer},
            device_id_type=mesh_id,
        )

    def own_back(l, c):
        return pltpu.make_async_copy(
            slot_sum.at[l, block_of(me), chunk_of(c)],
            back.at[l, block_of(me), chunk_of(c)],
            back_recv.at[l, c, 0],
        )

    def send_back(l):
        @pl.loop(0, n_chunks)
        def _(c):
            part_copy(l, c).wait_recv()
            cols = chunk_of(c)
            slot_sum[l, :, cols] = (near_sum[l, :, cols] + far_got[l, :, cols].astype(f32)).astype(bf16)
            for step in range(n_peers - 1, 0, -1):
                back_copy(l, c, step).start()
            own_back(l, c).start()

    last = n_local - 1
    for l in range(n_local):
        relay(0, l, distant)
        relay(1, l, distant)
        if l == 0:
            for copy in own_weights:
                copy.wait()
            for swap in swaps:
                swap.wait_recv()
        ratio_of(near_rows, 0, l)
    for l in range(n_local):
        wait_far(0, l)
        wait_far(1, l)
        if l == 0:
            ratio_of(far_rows, 1, l)
        relay(2, l, distant)
        if l > 0:
            ratio_of(far_rows, 1, l)
        near_part(l)
        if l > 0:
            send_back(l - 1)
        wait_far(2, l)
        far_part(l)
    send_back(last)

    for l in range(n_local):
        at = lax.broadcasted_iota(jnp.int32, (tokens, rows), 1) + l * rows
        pick = jnp.where(at == slot_col[...], 1.0, 0.0).astype(bf16)
        for c in range(n_chunks):
            own_back(l, c).wait()
            for step in range(1, n_peers):
                back_copy(l, c, step).wait_recv()
        term = jnp.dot(pick, back[l], preferred_element_type=f32)
        if l == 0:
            near_sum[0] = term
        else:
            near_sum[0] += term
    out[...] = (layer[...] + scale[...] * near_sum[0]).astype(bf16)

    for swap in swaps:
        swap.wait_send()
    for l in range(n_local):
        for a in range(3):
            for step in range(n_peers):
                if step:
                    row_copy(a, l, step).wait_send()
                hop_copy(a, l, step).wait_send()
        for c in range(n_chunks):
            part_copy(l, c).wait_send()
            for step in range(1, n_peers):
                back_copy(l, c, step).wait_send()


def whole_pass(
    state, base_state, keys, queries, mults, length, slots, gate, gain, w_in, w_out_t, value, n_peers, n_dp, cap
):
    tokens, width = state.shape
    n_local, _, part = w_in.shape
    w_in, w_out_t = jnp.swapaxes(w_in, 1, 2), jnp.swapaxes(w_out_t, 1, 2)
    rows = n_peers * cap
    chunk = width // 4
    n_chunks = width // chunk
    bf16, f32 = jnp.bfloat16, jnp.float32
    dma = pltpu.SemaphoreType.DMA
    vmem = pl.BlockSpec(memory_space=pltpu.VMEM)
    anyw = pl.BlockSpec(memory_space=pl.ANY)
    wide = (n_local, rows, width)
    return pl.pallas_call(
        functools.partial(whole_kernel, n_peers, n_dp, cap, chunk),
        out_shape=jax.ShapeDtypeStruct((tokens, width), bf16),
        in_specs=[vmem] * 7 + [anyw] * 6,
        out_specs=vmem,
        scratch_shapes=[
            pltpu.VMEM(keys.shape, bf16),
            pltpu.VMEM(queries.shape, bf16),
            pltpu.VMEM(mults.shape, bf16),
            pltpu.VMEM(value.shape, bf16),
            pltpu.VMEM((tokens, width), bf16),
            pltpu.VMEM((tokens, width), f32),
            pltpu.VMEM((tokens, width), f32),
            pltpu.VMEM((3, *wide), bf16),
            pltpu.VMEM((2, n_local, part, width), bf16),
            pltpu.VMEM((2, n_local, part, width), bf16),
            pltpu.VMEM((3, *wide), bf16),
            pltpu.VMEM((3, *wide), bf16),
            pltpu.VMEM((2, n_local, 2, rows, part), f32),
            pltpu.VMEM((2, rows, part), bf16),
            pltpu.VMEM(wide, f32),
            pltpu.VMEM(wide, bf16),
            pltpu.VMEM(wide, bf16),
            pltpu.VMEM(wide, bf16),
            pltpu.VMEM(wide, bf16),
            dma((4,)),
            dma((2,)),
            dma((2,)),
            dma((2,)),
            dma((3, n_local, n_peers)),
            dma((3, n_local, n_peers)),
            dma((3, n_local, n_peers)),
            dma((3, n_local, n_peers)),
            dma((n_local, n_chunks)),
            dma((n_local, n_chunks)),
            dma((n_local, n_chunks, n_peers)),
            dma((n_local, n_chunks, n_peers)),
        ],
        compiler_params=pltpu.CompilerParams(
            collective_id=0, has_side_effects=True, vmem_limit_bytes=60 * 1024 * 1024
        ),
        name="whole_pass",
    )(
        state,
        base_state,
        slots[None, :],
        slots[:, None],
        gate[:, None],
        gain[None, :],
        length[None, None],
        keys,
        queries,
        mults,
        value,
        w_in,
        w_out_t,
    )


def plain_pass(sent, w_in, w_out_t, n_peers, n_dp):
    near = 2 if n_dp % 2 == 0 else 1
    shards = [(w_in, w_out_t)]
    if near == 2:
        swap = [(i, i ^ 1) for i in range(n_dp)]
        shards.append((lax.ppermute(w_in, "dp", swap), lax.ppermute(w_out_t, "dp", swap)))
    own_rows = tuple(
        lax.all_to_all(a, "expert", split_axis=0, concat_axis=1, tiled=True) for a in sent
    )

    def partial_sum(rows):
        total = expert_terms(*rows, *shards[0])
        for part in shards[1:]:
            total = total + expert_terms(*rows, *part)
        return total

    far = n_dp // near
    far_rows = []
    for hop in range(1, far):
        ahead = [(i, (i + hop * near) % n_dp) for i in range(n_dp)]
        far_rows.append(tuple(lax.ppermute(a, "dp", ahead) for a in own_rows))
    slot_mult = partial_sum(own_rows)
    for hop in range(1, far):
        back = [((i + hop * near) % n_dp, i) for i in range(n_dp)]
        far_part = partial_sum(far_rows[hop - 1]).astype(jnp.bfloat16)
        slot_mult = slot_mult + lax.ppermute(far_part, "dp", back).astype(jnp.float32)

    return lax.all_to_all(
        slot_mult.astype(jnp.bfloat16), "expert", split_axis=1, concat_axis=0, tiled=True
    )


def body(
    enc_state,
    baseline,
    enc_keys,
    dec_queries,
    out_mult,
    doc_lengths,
    expert_ids,
    slot_ids,
    gate_prob,
    norm_gain,
    w_in,
    w_out_t,
    w_value,
):
    enc_len = enc_state.shape[2]
    feature_width = enc_state.shape[3]
    local_experts = w_in.shape[0]
    n_experts = local_experts * lax.axis_size("expert")
    n_dp = lax.axis_size("dp")
    capacity = max(2, 2 * enc_len // n_experts)

    n_peers = lax.axis_size("expert")
    if n_dp == 4 and local_experts == 2 and capacity % 16 == 0 and n_peers & (n_peers - 1) == 0 and feature_width % 512 == 0:
        expert = expert_ids[0, 0]
        slots = (
            lax.rem(expert, local_experts) * (n_peers * capacity)
            + (expert // local_experts) * capacity
            + slot_ids[0, 0]
        )
        return whole_pass(
            enc_state[0, 0],
            baseline[0, 0],
            enc_keys[0, 0],
            dec_queries[0, 0],
            out_mult[0, 0],
            doc_lengths[0, 0],
            slots,
            gate_prob[0, 0],
            norm_gain,
            w_in,
            w_out_t,
            w_value,
            n_peers,
            n_dp,
            capacity,
        )[None, None]

    tokens = enc_state[0, 0].astype(jnp.float32)
    row_scale = norm_gain * lax.rsqrt(jnp.mean(tokens * tokens, axis=-1, keepdims=True) + 1e-06)
    inputs = (tokens * row_scale).astype(jnp.bfloat16)
    base_inputs = (baseline[0, 0].astype(jnp.float32) * row_scale).astype(jnp.bfloat16)
    flat_slot = expert_ids[0, 0] * capacity + slot_ids[0, 0]
    onehot = (
        flat_slot[None, :] == jnp.arange(n_experts * capacity, dtype=jnp.int32)[:, None]
    ).astype(jnp.bfloat16)

    def dispatch(values):
        placed = jnp.dot(onehot, values, preferred_element_type=jnp.float32).astype(jnp.bfloat16)
        return placed.reshape(n_experts, capacity, feature_width)

    layer_mult = attend(
        dec_queries[0, 0], enc_keys[0, 0], out_mult[0, 0], doc_lengths[0, 0], w_value
    )
    scaled_mult = (gate_prob[0, 0][:, None] * layer_mult).astype(jnp.bfloat16)
    sent = (dispatch(inputs), dispatch(base_inputs), dispatch(scaled_mult))
    returned = plain_pass(sent, w_in, w_out_t, n_peers, n_dp)
    per_token = lax.dot_general(
        onehot,
        returned.reshape(n_experts * capacity, feature_width),
        (((0,), (0,)), ((), ())),
        preferred_element_type=jnp.float32,
    )
    result = (layer_mult + row_scale * per_token).astype(jnp.bfloat16)
    return result[None, None]


def solution(mesh):
    in_specs = (
        P("dp", "expert", None, None),
        P("dp", "expert", None, None),
        P("dp", "expert", None, None),
        P("dp", "expert", None, None),
        P("dp", "expert", None, None),
        P("dp", "expert"),
        P("dp", "expert", None),
        P("dp", "expert", None),
        P("dp", "expert", None),
        P(),
        P("expert", None, "dp"),
        P("expert", None, "dp"),
        P(),
    )
    out_specs = P("dp", "expert", None, None)
    return jax.shard_map(body, mesh=mesh, in_specs=in_specs, out_specs=out_specs, check_vma=False)
```

```python
import functools
import math

import jax
import jax.numpy as jnp
from jax import lax
from jax.experimental import pallas as pl
from jax.experimental.pallas import tpu as pltpu
from jax.sharding import PartitionSpec as P

HEADS = 16
HEAD_DIM = 64


def rescale(pre_act, base_act):
    upper_part = jnp.maximum(jnp.maximum(pre_act, base_act), 0.0)
    lower_part = jnp.maximum(-jnp.minimum(pre_act, base_act), 0.0)
    return upper_part / (upper_part + lower_part + jnp.where(upper_part > 0.0, 0.0, 1.0))


def attend(query_rows, key_rows, mult_rows, length, w_value):
    enc_len = key_rows.shape[0]
    dec_len = query_rows.shape[0]
    queries = query_rows.reshape(dec_len, HEADS, HEAD_DIM)
    keys = key_rows.reshape(enc_len, HEADS, HEAD_DIM)
    mults = mult_rows.reshape(dec_len, HEADS, HEAD_DIM)
    scores = jnp.einsum("qhd,khd->hqk", queries, keys, preferred_element_type=jnp.float32) * (
        1.0 / math.sqrt(HEAD_DIM)
    )
    valid = jnp.arange(enc_len, dtype=jnp.int32) < length
    scores = jnp.where(valid[None, None, :], scores, -jnp.inf)
    top_score = jnp.max(scores, axis=-1, keepdims=True)
    expo = jnp.exp(scores - top_score)
    attn = (expo / jnp.sum(expo, axis=-1, keepdims=True)).astype(jnp.bfloat16)
    value_mult = jnp.einsum("hqk,qhd->khd", attn, mults, preferred_element_type=jnp.float32).astype(
        jnp.bfloat16
    )
    return lax.dot_general(
        value_mult.reshape(enc_len, HEADS * HEAD_DIM),
        w_value,
        (((1,), (1,)), ((), ())),
        preferred_element_type=jnp.float32,
    )


def expert_terms(rows_in, rows_base, rows_mult, part_in, part_out):
    pre_act = jnp.einsum("erd,edf->erf", rows_in, part_in, preferred_element_type=jnp.float32)
    base_act = jnp.einsum("erd,edf->erf", rows_base, part_in, preferred_element_type=jnp.float32)
    hidden_mult = jnp.einsum(
        "erd,edf->erf", rows_mult, part_out, preferred_element_type=jnp.float32
    )
    act_mult = (rescale(pre_act, base_act) * hidden_mult).astype(jnp.bfloat16)
    return jnp.einsum("erf,edf->erd", act_mult, part_in, preferred_element_type=jnp.float32)


def times_t(left, right):
    return lax.dot_general(left, right, (((1,), (1,)), ((), ())), preferred_element_type=jnp.float32)


def whole_kernel(
    n_peers,
    n_dp,
    cap,
    chunk,
    state,
    base_state,
    expert_row,
    place_row,
    gate,
    gain,
    length,
    keys_at,
    queries_at,
    mults_at,
    value_at,
    w_in,
    w_out,
    out,
    keys,
    queries,
    mults,
    value,
    value_mult,
    layer,
    scale,
    sends,
    all_in,
    all_out,
    near_rows,
    far_rows,
    ratio,
    act,
    near_sum,
    far_sum,
    far_got,
    slot_sum,
    back,
    load_sem,
    weight_sem,
    swap_send,
    swap_recv,
    row_send,
    row_recv,
    hop_send,
    hop_recv,
    part_send,
    part_recv,
    back_send,
    back_recv,
):
    n_local = w_in.shape[0]
    tokens, width = state.shape
    rows = n_peers * cap
    n_chunks = width // chunk
    bf16, f32 = jnp.bfloat16, jnp.float32
    me = lax.axis_index("expert")
    dp = lax.axis_index("dp")
    pair = dp + 1 - 2 * lax.rem(dp, 2)
    across = lax.rem(dp + 2, n_dp)
    mesh_id = pl.DeviceIdType.MESH

    loads = []
    for at, (ref, held) in enumerate(
        ((queries_at, queries), (keys_at, keys), (mults_at, mults), (value_at, value))
    ):
        copy = pltpu.make_async_copy(ref, held, load_sem.at[at])
        copy.start()
        loads.append(copy)
    own_weights = []
    for at, (ref, held) in enumerate(((w_in, all_in), (w_out, all_out))):
        copy = pltpu.make_async_copy(ref, held.at[0], weight_sem.at[at])
        copy.start()
        own_weights.append(copy)

    def peer_at(step):
        peer, bit = 0, 1
        while bit < n_peers:
            digit = lax.rem(me // bit, 2)
            peer = peer + bit * (1 - digit if step & bit else digit)
            bit *= 2
        return peer

    barrier = pltpu.get_barrier_semaphore()
    for step in range(1, n_peers):
        pl.semaphore_signal(barrier, inc=1, device_id={"expert": peer_at(step)}, device_id_type=mesh_id)
    for other in (pair, across):
        pl.semaphore_signal(barrier, inc=1, device_id={"dp": other}, device_id_type=mesh_id)

    expert = expert_row[...]
    slot_row = (
        lax.rem(expert, n_local) * rows + lax.div(expert, n_local) * cap + place_row[...]
    )

    def column(row):
        return jnp.transpose(jnp.broadcast_to(row, (128, tokens)))[:, :1]

    def place_rows(a, l, values):
        at = lax.broadcasted_iota(jnp.int32, (rows, tokens), 0) + l * rows
        onehot = jnp.where(at == slot_row, 1.0, 0.0).astype(bf16)
        sends[a, l] = jnp.dot(onehot, values, preferred_element_type=f32).astype(bf16)

    def block_of(src):
        return pl.ds(pl.multiple_of(src * cap, cap), cap)

    def row_copy(a, l, step):
        peer = peer_at(step)
        return pltpu.make_async_remote_copy(
            src_ref=sends.at[a, l, block_of(peer), :],
            dst_ref=near_rows.at[a, l, block_of(me), :],
            send_sem=row_send.at[a, l, step],
            recv_sem=row_recv.at[a, l, step],
            device_id={"expert": peer},
            device_id_type=mesh_id,
        )

    def own_copy(a, l):
        return pltpu.make_async_copy(
            sends.at[a, l, block_of(me), :], near_rows.at[a, l, block_of(me), :], row_recv.at[a, l, 0]
        )

    def send_rows(a, l):
        own_copy(a, l).start()
        for step in range(n_peers - 1, 0, -1):
            row_copy(a, l, step).start()

    def hop_copy(a, l, step):
        src = block_of(peer_at(step))
        return pltpu.make_async_remote_copy(
            src_ref=near_rows.at[a, l, src, :],
            dst_ref=far_rows.at[a, l, src, :],
            send_sem=hop_send.at[a, l, step],
            recv_sem=hop_recv.at[a, l, step],
            device_id={"dp": across},
            device_id_type=mesh_id,
        )

    def relay(a, l, steps):
        for step in steps:
            if step == 0:
                own_copy(a, l).wait()
            else:
                row_copy(a, l, step).wait_recv()
            hop_copy(a, l, step).start()

    def wait_far(a, l):
        for step in range(n_peers):
            hop_copy(a, l, step).wait_recv()

    close = range(0, 2)
    distant = range(2, n_peers)

    token_rows = state[...].astype(f32)
    scale[...] = gain[...] * lax.rsqrt(
        jnp.mean(token_rows * token_rows, axis=-1, keepdims=True) + 1e-06
    )
    inputs = (token_rows * scale[...]).astype(bf16)
    place_rows(0, 0, inputs)
    pl.semaphore_wait(barrier, n_peers + 1)
    send_rows(0, 0)
    base_inputs = (base_state[...].astype(f32) * scale[...]).astype(bf16)
    place_rows(1, 0, base_inputs)
    send_rows(1, 0)
    for l in range(1, n_local):
        place_rows(0, l, inputs)
        send_rows(0, l)
        place_rows(1, l, base_inputs)
        send_rows(1, l)

    swaps = []
    for at, (ref, held) in enumerate(((w_in, all_in), (w_out, all_out))):
        swap = pltpu.make_async_remote_copy(
            src_ref=ref,
            dst_ref=held.at[1],
            send_sem=swap_send.at[at],
            recv_sem=swap_recv.at[at],
            device_id={"dp": pair},
            device_id_type=mesh_id,
        )
        swap.start()
        swaps.append(swap)

    for l in range(n_local):
        for a in range(2):
            relay(a, l, close)

    for copy in loads:
        copy.wait()

    def two_heads(both):
        cols = pl.ds(pl.multiple_of(both * 2 * HEAD_DIM, 2 * HEAD_DIM), 2 * HEAD_DIM)
        query, key, mult = queries[:, cols], keys[:, cols], mults[:, cols]
        first = lax.broadcasted_iota(jnp.int32, query.shape, 1) < HEAD_DIM
        zero = jnp.zeros_like(query)
        found = []
        for head in range(2):
            mine = jnp.where(first, query, zero) if head == 0 else jnp.where(first, zero, query)
            scores = times_t(key, mine) * (1.0 / math.sqrt(HEAD_DIM))
            at = lax.broadcasted_iota(jnp.int32, scores.shape, 0)
            scores = jnp.where(at < length[...], scores, -jnp.inf)
            expo = jnp.exp(scores - jnp.max(scores, axis=0, keepdims=True))
            attn = (expo / jnp.sum(expo, axis=0, keepdims=True)).astype(bf16)
            found.append(jnp.dot(attn, mult, preferred_element_type=f32))
        left = lax.broadcasted_iota(jnp.int32, found[0].shape, 1) < HEAD_DIM
        value_mult[:, cols] = jnp.where(left, found[0], found[1]).astype(bf16)

    pieces = width // (2 * HEAD_DIM)
    bounds = [pieces * at // 4 for at in range(5)]
    for at in range(4):
        pl.loop(bounds[at], bounds[at + 1])(two_heads)
        if at < 2:
            relay(at, 0, distant)

    def chunk_of(c):
        return pl.ds(pl.multiple_of(c * chunk, chunk), chunk)

    @pl.loop(0, n_chunks)
    def _(c):
        layer[:, chunk_of(c)] = times_t(value_mult[...], value[chunk_of(c), :])

    scaled = (column(gate[...]) * layer[...]).astype(bf16)
    for l in range(n_local):
        place_rows(2, l, scaled)
        send_rows(2, l)
    for l in range(n_local):
        relay(2, l, close)

    def ratio_of(buf, half, l):
        @pl.loop(0, 2)
        def _(shard):
            weight = all_in[shard, l]
            pre = times_t(buf[0, l], weight)
            base = times_t(buf[1, l], weight)
            ratio[half, l, shard] = rescale(pre, base)

    def acts_of(buf, half, l):
        @pl.loop(0, 2)
        def _(shard):
            hidden = times_t(buf[2, l], all_out[shard, l])
            act[shard] = (ratio[half, l, shard] * hidden).astype(bf16)

    def chunk_sum(l, c):
        cols = chunk_of(c)
        return jnp.dot(act[0], all_in[0, l, :, cols], preferred_element_type=f32) + jnp.dot(
            act[1], all_in[1, l, :, cols], preferred_element_type=f32
        )

    def part_copy(l, c):
        return pltpu.make_async_remote_copy(
            src_ref=far_sum.at[l, :, chunk_of(c)],
            dst_ref=far_got.at[l, :, chunk_of(c)],
            send_sem=part_send.at[l, c],
            recv_sem=part_recv.at[l, c],
            device_id={"dp": across},
            device_id_type=mesh_id,
        )

    def near_part(l):
        acts_of(near_rows, 0, l)

        @pl.loop(0, n_chunks)
        def _(c):
            near_sum[l, :, chunk_of(c)] = chunk_sum(l, c)

    def far_part(l):
        acts_of(far_rows, 1, l)

        @pl.loop(0, n_chunks)
        def _(c):
            far_sum[l, :, chunk_of(c)] = chunk_sum(l, c).astype(bf16)
            part_copy(l, c).start()

    def back_copy(l, c, step):
        peer = peer_at(step)
        return pltpu.make_async_remote_copy(
            src_ref=slot_sum.at[l, block_of(peer), chunk_of(c)],
            dst_ref=back.at[l, block_of(me), chunk_of(c)],
            send_sem=back_send.at[l, c, step],
            recv_sem=back_recv.at[l, c, step],
            device_id={"expert": peer},
            device_id_type=mesh_id,
        )

    def own_back(l, c):
        return pltpu.make_async_copy(
            slot_sum.at[l, block_of(me), chunk_of(c)],
            back.at[l, block_of(me), chunk_of(c)],
            back_recv.at[l, c, 0],
        )

    def send_back(l):
        @pl.loop(0, n_chunks)
        def _(c):
            part_copy(l, c).wait_recv()
            cols = chunk_of(c)
            slot_sum[l, :, cols] = (near_sum[l, :, cols] + far_got[l, :, cols].astype(f32)).astype(bf16)
            for step in range(n_peers - 1, 0, -1):
                back_copy(l, c, step).start()
            own_back(l, c).start()

    last = n_local - 1
    for l in range(n_local):
        if l > 0:
            relay(0, l, distant)
            relay(1, l, distant)
        if l == 0:
            for copy in own_weights:
                copy.wait()
            for swap in swaps:
                swap.wait_recv()
        ratio_of(near_rows, 0, l)
    for l in range(n_local):
        wait_far(0, l)
        wait_far(1, l)
        if l == 0:
            ratio_of(far_rows, 1, l)
        relay(2, l, distant)
        if l > 0:
            ratio_of(far_rows, 1, l)
        near_part(l)
        if l > 0:
            send_back(l - 1)
        wait_far(2, l)
        far_part(l)
    send_back(last)

    slot_col = column(slot_row.astype(f32))
    for l in range(n_local):
        at = lax.broadcasted_iota(jnp.int32, (tokens, rows), 1) + l * rows
        pick = jnp.where(at.astype(f32) == slot_col, 1.0, 0.0).astype(bf16)
        for c in range(n_chunks):
            own_back(l, c).wait()
            for step in range(1, n_peers):
                back_copy(l, c, step).wait_recv()
        term = jnp.dot(pick, back[l], preferred_element_type=f32)
        if l == 0:
            near_sum[0] = term
        else:
            near_sum[0] += term
    out[...] = (layer[...] + scale[...] * near_sum[0]).astype(bf16)

    for swap in swaps:
        swap.wait_send()
    for l in range(n_local):
        for a in range(3):
            for step in range(n_peers):
                if step:
                    row_copy(a, l, step).wait_send()
                hop_copy(a, l, step).wait_send()
        for c in range(n_chunks):
            part_copy(l, c).wait_send()
            for step in range(1, n_peers):
                back_copy(l, c, step).wait_send()


def whole_pass(
    state, base_state, keys, queries, mults, length, expert, place, gate, gain, w_in, w_out_t, value, n_peers, n_dp, cap
):
    tokens, width = state.shape
    n_local, _, part = w_in.shape
    w_in, w_out_t = jnp.swapaxes(w_in, 1, 2), jnp.swapaxes(w_out_t, 1, 2)
    rows = n_peers * cap
    chunk = width // 4
    n_chunks = width // chunk
    bf16, f32 = jnp.bfloat16, jnp.float32
    dma = pltpu.SemaphoreType.DMA
    vmem = pl.BlockSpec(memory_space=pltpu.VMEM)
    anyw = pl.BlockSpec(memory_space=pl.ANY)
    wide = (n_local, rows, width)
    return pl.pallas_call(
        functools.partial(whole_kernel, n_peers, n_dp, cap, chunk),
        out_shape=jax.ShapeDtypeStruct((tokens, width), bf16),
        in_specs=[vmem] * 7 + [anyw] * 6,
        out_specs=vmem,
        scratch_shapes=[
            pltpu.VMEM(keys.shape, bf16),
            pltpu.VMEM(queries.shape, bf16),
            pltpu.VMEM(mults.shape, bf16),
            pltpu.VMEM(value.shape, bf16),
            pltpu.VMEM((tokens, width), bf16),
            pltpu.VMEM((tokens, width), f32),
            pltpu.VMEM((tokens, width), f32),
            pltpu.VMEM((3, *wide), bf16),
            pltpu.VMEM((2, n_local, part, width), bf16),
            pltpu.VMEM((2, n_local, part, width), bf16),
            pltpu.VMEM((3, *wide), bf16),
            pltpu.VMEM((3, *wide), bf16),
            pltpu.VMEM((2, n_local, 2, rows, part), f32),
            pltpu.VMEM((2, rows, part), bf16),
            pltpu.VMEM(wide, f32),
            pltpu.VMEM(wide, bf16),
            pltpu.VMEM(wide, bf16),
            pltpu.VMEM(wide, bf16),
            pltpu.VMEM(wide, bf16),
            dma((4,)),
            dma((2,)),
            dma((2,)),
            dma((2,)),
            dma((3, n_local, n_peers)),
            dma((3, n_local, n_peers)),
            dma((3, n_local, n_peers)),
            dma((3, n_local, n_peers)),
            dma((n_local, n_chunks)),
            dma((n_local, n_chunks)),
            dma((n_local, n_chunks, n_peers)),
            dma((n_local, n_chunks, n_peers)),
        ],
        compiler_params=pltpu.CompilerParams(
            collective_id=0, has_side_effects=True, vmem_limit_bytes=60 * 1024 * 1024
        ),
        name="whole_pass",
    )(
        state,
        base_state,
        expert,
        place,
        gate,
        gain[None, :],
        length,
        keys,
        queries,
        mults,
        value,
        w_in,
        w_out_t,
    )


def plain_pass(sent, w_in, w_out_t, n_peers, n_dp):
    near = 2 if n_dp % 2 == 0 else 1
    shards = [(w_in, w_out_t)]
    if near == 2:
        swap = [(i, i ^ 1) for i in range(n_dp)]
        shards.append((lax.ppermute(w_in, "dp", swap), lax.ppermute(w_out_t, "dp", swap)))
    own_rows = tuple(
        lax.all_to_all(a, "expert", split_axis=0, concat_axis=1, tiled=True) for a in sent
    )

    def partial_sum(rows):
        total = expert_terms(*rows, *shards[0])
        for part in shards[1:]:
            total = total + expert_terms(*rows, *part)
        return total

    far = n_dp // near
    far_rows = []
    for hop in range(1, far):
        ahead = [(i, (i + hop * near) % n_dp) for i in range(n_dp)]
        far_rows.append(tuple(lax.ppermute(a, "dp", ahead) for a in own_rows))
    slot_mult = partial_sum(own_rows)
    for hop in range(1, far):
        back = [((i + hop * near) % n_dp, i) for i in range(n_dp)]
        far_part = partial_sum(far_rows[hop - 1]).astype(jnp.bfloat16)
        slot_mult = slot_mult + lax.ppermute(far_part, "dp", back).astype(jnp.float32)

    return lax.all_to_all(
        slot_mult.astype(jnp.bfloat16), "expert", split_axis=1, concat_axis=0, tiled=True
    )


def body(
    enc_state,
    baseline,
    enc_keys,
    dec_queries,
    out_mult,
    doc_lengths,
    expert_ids,
    slot_ids,
    gate_prob,
    norm_gain,
    w_in,
    w_out_t,
    w_value,
):
    enc_len = enc_state.shape[2]
    feature_width = enc_state.shape[3]
    local_experts = w_in.shape[0]
    n_experts = local_experts * lax.axis_size("expert")
    n_dp = lax.axis_size("dp")
    capacity = max(2, 2 * enc_len // n_experts)

    n_peers = lax.axis_size("expert")
    if n_dp == 4 and local_experts == 2 and capacity % 16 == 0 and n_peers & (n_peers - 1) == 0 and feature_width % 512 == 0:
        return whole_pass(
            enc_state[0, 0],
            baseline[0, 0],
            enc_keys[0, 0],
            dec_queries[0, 0],
            out_mult[0, 0],
            doc_lengths,
            expert_ids[0],
            slot_ids[0],
            gate_prob[0],
            norm_gain,
            w_in,
            w_out_t,
            w_value,
            n_peers,
            n_dp,
            capacity,
        )[None, None]

    tokens = enc_state[0, 0].astype(jnp.float32)
    row_scale = norm_gain * lax.rsqrt(jnp.mean(tokens * tokens, axis=-1, keepdims=True) + 1e-06)
    inputs = (tokens * row_scale).astype(jnp.bfloat16)
    base_inputs = (baseline[0, 0].astype(jnp.float32) * row_scale).astype(jnp.bfloat16)
    flat_slot = expert_ids[0, 0] * capacity + slot_ids[0, 0]
    onehot = (
        flat_slot[None, :] == jnp.arange(n_experts * capacity, dtype=jnp.int32)[:, None]
    ).astype(jnp.bfloat16)

    def dispatch(values):
        placed = jnp.dot(onehot, values, preferred_element_type=jnp.float32).astype(jnp.bfloat16)
        return placed.reshape(n_experts, capacity, feature_width)

    layer_mult = attend(
        dec_queries[0, 0], enc_keys[0, 0], out_mult[0, 0], doc_lengths[0, 0], w_value
    )
    scaled_mult = (gate_prob[0, 0][:, None] * layer_mult).astype(jnp.bfloat16)
    sent = (dispatch(inputs), dispatch(base_inputs), dispatch(scaled_mult))
    returned = plain_pass(sent, w_in, w_out_t, n_peers, n_dp)
    per_token = lax.dot_general(
        onehot,
        returned.reshape(n_experts * capacity, feature_width),
        (((0,), (0,)), ((), ())),
        preferred_element_type=jnp.float32,
    )
    result = (layer_mult + row_scale * per_token).astype(jnp.bfloat16)
    return result[None, None]


def solution(mesh):
    in_specs = (
        P("dp", "expert", None, None),
        P("dp", "expert", None, None),
        P("dp", "expert", None, None),
        P("dp", "expert", None, None),
        P("dp", "expert", None, None),
        P("dp", "expert"),
        P("dp", "expert", None),
        P("dp", "expert", None),
        P("dp", "expert", None),
        P(),
        P("expert", None, "dp"),
        P("expert", None, "dp"),
        P(),
    )
    out_specs = P("dp", "expert", None, None)
    return jax.shard_map(body, mesh=mesh, in_specs=in_specs, out_specs=out_specs, check_vma=False)
```

```python
import functools
import math

import jax
import jax.numpy as jnp
from jax import lax
from jax.experimental import pallas as pl
from jax.experimental.pallas import tpu as pltpu
from jax.sharding import PartitionSpec as P

HEADS = 16
HEAD_DIM = 64


def rescale(pre_act, base_act):
    upper_part = jnp.maximum(jnp.maximum(pre_act, base_act), 0.0)
    lower_part = jnp.maximum(-jnp.minimum(pre_act, base_act), 0.0)
    return upper_part / (upper_part + lower_part + jnp.where(upper_part > 0.0, 0.0, 1.0))


def attend(query_rows, key_rows, mult_rows, length, w_value):
    enc_len = key_rows.shape[0]
    dec_len = query_rows.shape[0]
    queries = query_rows.reshape(dec_len, HEADS, HEAD_DIM)
    keys = key_rows.reshape(enc_len, HEADS, HEAD_DIM)
    mults = mult_rows.reshape(dec_len, HEADS, HEAD_DIM)
    scores = jnp.einsum("qhd,khd->hqk", queries, keys, preferred_element_type=jnp.float32) * (
        1.0 / math.sqrt(HEAD_DIM)
    )
    valid = jnp.arange(enc_len, dtype=jnp.int32) < length
    scores = jnp.where(valid[None, None, :], scores, -jnp.inf)
    top_score = jnp.max(scores, axis=-1, keepdims=True)
    expo = jnp.exp(scores - top_score)
    attn = (expo / jnp.sum(expo, axis=-1, keepdims=True)).astype(jnp.bfloat16)
    value_mult = jnp.einsum("hqk,qhd->khd", attn, mults, preferred_element_type=jnp.float32).astype(
        jnp.bfloat16
    )
    return lax.dot_general(
        value_mult.reshape(enc_len, HEADS * HEAD_DIM),
        w_value,
        (((1,), (1,)), ((), ())),
        preferred_element_type=jnp.float32,
    )


def expert_terms(rows_in, rows_base, rows_mult, part_in, part_out):
    pre_act = jnp.einsum("erd,edf->erf", rows_in, part_in, preferred_element_type=jnp.float32)
    base_act = jnp.einsum("erd,edf->erf", rows_base, part_in, preferred_element_type=jnp.float32)
    hidden_mult = jnp.einsum(
        "erd,edf->erf", rows_mult, part_out, preferred_element_type=jnp.float32
    )
    act_mult = (rescale(pre_act, base_act) * hidden_mult).astype(jnp.bfloat16)
    return jnp.einsum("erf,edf->erd", act_mult, part_in, preferred_element_type=jnp.float32)


def times_t(left, right):
    return lax.dot_general(left, right, (((1,), (1,)), ((), ())), preferred_element_type=jnp.float32)


def whole_kernel(
    n_peers,
    n_dp,
    cap,
    chunk,
    state,
    base_state,
    expert_row,
    place_row,
    gate,
    gain,
    length,
    keys_at,
    queries_at,
    mults_at,
    value_at,
    w_in,
    w_out,
    out,
    keys,
    queries,
    mults,
    value,
    value_mult,
    layer,
    scale,
    sends,
    all_in,
    all_out,
    near_rows,
    far_rows,
    ratio,
    act,
    near_sum,
    far_sum,
    far_got,
    slot_sum,
    back,
    load_sem,
    weight_sem,
    swap_send,
    swap_recv,
    row_send,
    row_recv,
    hop_send,
    hop_recv,
    part_send,
    part_recv,
    back_send,
    back_recv,
):
    n_local = w_in.shape[0]
    tokens, width = state.shape
    rows = n_peers * cap
    n_chunks = width // chunk
    bf16, f32 = jnp.bfloat16, jnp.float32
    me = lax.axis_index("expert")
    dp = lax.axis_index("dp")
    pair = dp + 1 - 2 * lax.rem(dp, 2)
    across = lax.rem(dp + 2, n_dp)
    mesh_id = pl.DeviceIdType.MESH

    loads = []
    for at, (ref, held) in enumerate(
        ((queries_at, queries), (keys_at, keys), (mults_at, mults), (value_at, value))
    ):
        copy = pltpu.make_async_copy(ref, held, load_sem.at[at])
        copy.start()
        loads.append(copy)
    own_weights = []
    for at, (ref, held) in enumerate(((w_in, all_in), (w_out, all_out))):
        copy = pltpu.make_async_copy(ref, held.at[0], weight_sem.at[at])
        copy.start()
        own_weights.append(copy)

    def peer_at(step):
        peer, bit = 0, 1
        while bit < n_peers:
            digit = lax.rem(me // bit, 2)
            peer = peer + bit * (1 - digit if step & bit else digit)
            bit *= 2
        return peer

    barrier = pltpu.get_barrier_semaphore()
    for step in range(1, n_peers):
        pl.semaphore_signal(barrier, inc=1, device_id={"expert": peer_at(step)}, device_id_type=mesh_id)
    for other in (pair, across):
        pl.semaphore_signal(barrier, inc=1, device_id={"dp": other}, device_id_type=mesh_id)

    expert = expert_row[...]
    slot_row = (
        lax.rem(expert, n_local) * rows + lax.div(expert, n_local) * cap + place_row[...]
    )

    def column(row):
        return jnp.transpose(jnp.broadcast_to(row, (128, tokens)))[:, :1]

    def place_rows(a, l, values):
        at = lax.broadcasted_iota(jnp.int32, (rows, tokens), 0) + l * rows
        onehot = jnp.where(at == slot_row, 1.0, 0.0).astype(bf16)
        sends[a, l] = jnp.dot(onehot, values, preferred_element_type=f32).astype(bf16)

    def block_of(src):
        return pl.ds(pl.multiple_of(src * cap, cap), cap)

    def row_copy(a, l, step):
        peer = peer_at(step)
        return pltpu.make_async_remote_copy(
            src_ref=sends.at[a, l, block_of(peer), :],
            dst_ref=near_rows.at[a, l, block_of(me), :],
            send_sem=row_send.at[a, l, step],
            recv_sem=row_recv.at[a, l, step],
            device_id={"expert": peer},
            device_id_type=mesh_id,
        )

    def own_copy(a, l):
        return pltpu.make_async_copy(
            sends.at[a, l, block_of(me), :], near_rows.at[a, l, block_of(me), :], row_recv.at[a, l, 0]
        )

    def send_rows(a, l):
        own_copy(a, l).start()
        for step in range(n_peers - 1, 0, -1):
            row_copy(a, l, step).start()

    def hop_copy(a, l, step):
        src = block_of(peer_at(step))
        return pltpu.make_async_remote_copy(
            src_ref=near_rows.at[a, l, src, :],
            dst_ref=far_rows.at[a, l, src, :],
            send_sem=hop_send.at[a, l, step],
            recv_sem=hop_recv.at[a, l, step],
            device_id={"dp": across},
            device_id_type=mesh_id,
        )

    def relay(a, l, steps):
        for step in steps:
            if step == 0:
                own_copy(a, l).wait()
            else:
                row_copy(a, l, step).wait_recv()
            hop_copy(a, l, step).start()

    def wait_far(a, l):
        for step in range(n_peers):
            hop_copy(a, l, step).wait_recv()

    close = range(0, 2)
    distant = range(2, n_peers)

    token_rows = state[...].astype(f32)
    scale[...] = gain[...] * lax.rsqrt(
        jnp.mean(token_rows * token_rows, axis=-1, keepdims=True) + 1e-06
    )
    inputs = (token_rows * scale[...]).astype(bf16)
    place_rows(0, 0, inputs)
    pl.semaphore_wait(barrier, n_peers + 1)
    send_rows(0, 0)
    base_inputs = (base_state[...].astype(f32) * scale[...]).astype(bf16)
    place_rows(1, 0, base_inputs)
    send_rows(1, 0)
    for l in range(1, n_local):
        place_rows(0, l, inputs)
        send_rows(0, l)
        place_rows(1, l, base_inputs)

    swaps = []
    for at, (ref, held) in enumerate(((w_in, all_in), (w_out, all_out))):
        swap = pltpu.make_async_remote_copy(
            src_ref=ref,
            dst_ref=held.at[1],
            send_sem=swap_send.at[at],
            recv_sem=swap_recv.at[at],
            device_id={"dp": pair},
            device_id_type=mesh_id,
        )
        swap.start()
        swaps.append(swap)

    relay(0, 0, close)
    relay(1, 0, close)
    for l in range(1, n_local):
        relay(0, l, close)

    for copy in loads:
        copy.wait()

    def two_heads(both):
        cols = pl.ds(pl.multiple_of(both * 2 * HEAD_DIM, 2 * HEAD_DIM), 2 * HEAD_DIM)
        query, key, mult = queries[:, cols], keys[:, cols], mults[:, cols]
        first = lax.broadcasted_iota(jnp.int32, query.shape, 1) < HEAD_DIM
        zero = jnp.zeros_like(query)
        found = []
        for head in range(2):
            mine = jnp.where(first, query, zero) if head == 0 else jnp.where(first, zero, query)
            scores = times_t(key, mine) * (1.0 / math.sqrt(HEAD_DIM))
            at = lax.broadcasted_iota(jnp.int32, scores.shape, 0)
            scores = jnp.where(at < length[...], scores, -jnp.inf)
            expo = jnp.exp(scores - jnp.max(scores, axis=0, keepdims=True))
            attn = (expo / jnp.sum(expo, axis=0, keepdims=True)).astype(bf16)
            found.append(jnp.dot(attn, mult, preferred_element_type=f32))
        left = lax.broadcasted_iota(jnp.int32, found[0].shape, 1) < HEAD_DIM
        value_mult[:, cols] = jnp.where(left, found[0], found[1]).astype(bf16)

    pieces = width // (2 * HEAD_DIM)
    bounds = [pieces * at // 4 for at in range(5)]
    for at in range(4):
        pl.loop(bounds[at], bounds[at + 1])(two_heads)
        if at == 1:
            relay(0, 0, distant)

    def chunk_of(c):
        return pl.ds(pl.multiple_of(c * chunk, chunk), chunk)

    @pl.loop(0, n_chunks)
    def _(c):
        layer[:, chunk_of(c)] = times_t(value_mult[...], value[chunk_of(c), :])

    scaled = (column(gate[...]) * layer[...]).astype(bf16)
    for l in range(n_local):
        place_rows(2, l, scaled)
        if l > 0:
            send_rows(1, l)
        send_rows(2, l)
    for l in range(n_local):
        if l > 0:
            relay(1, l, close)
        relay(2, l, close)

    def ratio_of(buf, half, l):
        @pl.loop(0, 2)
        def _(shard):
            weight = all_in[shard, l]
            pre = times_t(buf[0, l], weight)
            base = times_t(buf[1, l], weight)
            ratio[half, l, shard] = rescale(pre, base)

    def acts_of(buf, half, l):
        @pl.loop(0, 2)
        def _(shard):
            hidden = times_t(buf[2, l], all_out[shard, l])
            act[shard] = (ratio[half, l, shard] * hidden).astype(bf16)

    def chunk_sum(l, c):
        cols = chunk_of(c)
        return jnp.dot(act[0], all_in[0, l, :, cols], preferred_element_type=f32) + jnp.dot(
            act[1], all_in[1, l, :, cols], preferred_element_type=f32
        )

    def part_copy(l, c):
        return pltpu.make_async_remote_copy(
            src_ref=far_sum.at[l, :, chunk_of(c)],
            dst_ref=far_got.at[l, :, chunk_of(c)],
            send_sem=part_send.at[l, c],
            recv_sem=part_recv.at[l, c],
            device_id={"dp": across},
            device_id_type=mesh_id,
        )

    def near_part(l):
        acts_of(near_rows, 0, l)

        @pl.loop(0, n_chunks)
        def _(c):
            near_sum[l, :, chunk_of(c)] = chunk_sum(l, c)

    def far_part(l):
        acts_of(far_rows, 1, l)

        @pl.loop(0, n_chunks)
        def _(c):
            far_sum[l, :, chunk_of(c)] = chunk_sum(l, c).astype(bf16)
            part_copy(l, c).start()

    def back_copy(l, c, step):
        peer = peer_at(step)
        return pltpu.make_async_remote_copy(
            src_ref=slot_sum.at[l, block_of(peer), chunk_of(c)],
            dst_ref=back.at[l, block_of(me), chunk_of(c)],
            send_sem=back_send.at[l, c, step],
            recv_sem=back_recv.at[l, c, step],
            device_id={"expert": peer},
            device_id_type=mesh_id,
        )

    def own_back(l, c):
        return pltpu.make_async_copy(
            slot_sum.at[l, block_of(me), chunk_of(c)],
            back.at[l, block_of(me), chunk_of(c)],
            back_recv.at[l, c, 0],
        )

    def send_back(l):
        @pl.loop(0, n_chunks)
        def _(c):
            part_copy(l, c).wait_recv()
            cols = chunk_of(c)
            slot_sum[l, :, cols] = (near_sum[l, :, cols] + far_got[l, :, cols].astype(f32)).astype(bf16)
            for step in range(n_peers - 1, 0, -1):
                back_copy(l, c, step).start()
            own_back(l, c).start()

    last = n_local - 1
    for l in range(n_local):
        if l > 1:
            relay(0, l, distant)
        relay(1, l, distant)
        if l == 0:
            for copy in own_weights:
                copy.wait()
            for swap in swaps:
                swap.wait_recv()
        ratio_of(near_rows, 0, l)
        if l == 0 and n_local > 1:
            relay(0, 1, distant)
        relay(2, l, distant)
        near_part(l)
        wait_far(0, l)
        wait_far(1, l)
        ratio_of(far_rows, 1, l)
        if l > 0:
            send_back(l - 1)
        wait_far(2, l)
        far_part(l)
    send_back(last)

    slot_col = column(slot_row.astype(f32))
    for l in range(n_local):
        at = lax.broadcasted_iota(jnp.int32, (tokens, rows), 1) + l * rows
        pick = jnp.where(at.astype(f32) == slot_col, 1.0, 0.0).astype(bf16)
        for c in range(n_chunks):
            own_back(l, c).wait()
            for step in range(1, n_peers):
                back_copy(l, c, step).wait_recv()
        term = jnp.dot(pick, back[l], preferred_element_type=f32)
        if l == 0:
            near_sum[0] = term
        else:
            near_sum[0] += term
    out[...] = (layer[...] + scale[...] * near_sum[0]).astype(bf16)

    for swap in swaps:
        swap.wait_send()
    for l in range(n_local):
        for a in range(3):
            for step in range(n_peers):
                if step:
                    row_copy(a, l, step).wait_send()
                hop_copy(a, l, step).wait_send()
        for c in range(n_chunks):
            part_copy(l, c).wait_send()
            for step in range(1, n_peers):
                back_copy(l, c, step).wait_send()


def whole_pass(
    state, base_state, keys, queries, mults, length, expert, place, gate, gain, w_in, w_out_t, value, n_peers, n_dp, cap
):
    tokens, width = state.shape
    n_local, _, part = w_in.shape
    w_in, w_out_t = jnp.swapaxes(w_in, 1, 2), jnp.swapaxes(w_out_t, 1, 2)
    rows = n_peers * cap
    chunk = width // 4
    n_chunks = width // chunk
    bf16, f32 = jnp.bfloat16, jnp.float32
    dma = pltpu.SemaphoreType.DMA
    vmem = pl.BlockSpec(memory_space=pltpu.VMEM)
    anyw = pl.BlockSpec(memory_space=pl.ANY)
    wide = (n_local, rows, width)
    return pl.pallas_call(
        functools.partial(whole_kernel, n_peers, n_dp, cap, chunk),
        out_shape=jax.ShapeDtypeStruct((tokens, width), bf16),
        in_specs=[vmem] * 7 + [anyw] * 6,
        out_specs=vmem,
        scratch_shapes=[
            pltpu.VMEM(keys.shape, bf16),
            pltpu.VMEM(queries.shape, bf16),
            pltpu.VMEM(mults.shape, bf16),
            pltpu.VMEM(value.shape, bf16),
            pltpu.VMEM((tokens, width), bf16),
            pltpu.VMEM((tokens, width), f32),
            pltpu.VMEM((tokens, width), f32),
            pltpu.VMEM((3, *wide), bf16),
            pltpu.VMEM((2, n_local, part, width), bf16),
            pltpu.VMEM((2, n_local, part, width), bf16),
            pltpu.VMEM((3, *wide), bf16),
            pltpu.VMEM((3, *wide), bf16),
            pltpu.VMEM((2, n_local, 2, rows, part), f32),
            pltpu.VMEM((2, rows, part), bf16),
            pltpu.VMEM(wide, f32),
            pltpu.VMEM(wide, bf16),
            pltpu.VMEM(wide, bf16),
            pltpu.VMEM(wide, bf16),
            pltpu.VMEM(wide, bf16),
            dma((4,)),
            dma((2,)),
            dma((2,)),
            dma((2,)),
            dma((3, n_local, n_peers)),
            dma((3, n_local, n_peers)),
            dma((3, n_local, n_peers)),
            dma((3, n_local, n_peers)),
            dma((n_local, n_chunks)),
            dma((n_local, n_chunks)),
            dma((n_local, n_chunks, n_peers)),
            dma((n_local, n_chunks, n_peers)),
        ],
        compiler_params=pltpu.CompilerParams(
            collective_id=0, has_side_effects=True, vmem_limit_bytes=60 * 1024 * 1024
        ),
        name="whole_pass",
    )(
        state,
        base_state,
        expert,
        place,
        gate,
        gain[None, :],
        length,
        keys,
        queries,
        mults,
        value,
        w_in,
        w_out_t,
    )


def plain_pass(sent, w_in, w_out_t, n_peers, n_dp):
    near = 2 if n_dp % 2 == 0 else 1
    shards = [(w_in, w_out_t)]
    if near == 2:
        swap = [(i, i ^ 1) for i in range(n_dp)]
        shards.append((lax.ppermute(w_in, "dp", swap), lax.ppermute(w_out_t, "dp", swap)))
    own_rows = tuple(
        lax.all_to_all(a, "expert", split_axis=0, concat_axis=1, tiled=True) for a in sent
    )

    def partial_sum(rows):
        total = expert_terms(*rows, *shards[0])
        for part in shards[1:]:
            total = total + expert_terms(*rows, *part)
        return total

    far = n_dp // near
    far_rows = []
    for hop in range(1, far):
        ahead = [(i, (i + hop * near) % n_dp) for i in range(n_dp)]
        far_rows.append(tuple(lax.ppermute(a, "dp", ahead) for a in own_rows))
    slot_mult = partial_sum(own_rows)
    for hop in range(1, far):
        back = [((i + hop * near) % n_dp, i) for i in range(n_dp)]
        far_part = partial_sum(far_rows[hop - 1]).astype(jnp.bfloat16)
        slot_mult = slot_mult + lax.ppermute(far_part, "dp", back).astype(jnp.float32)

    return lax.all_to_all(
        slot_mult.astype(jnp.bfloat16), "expert", split_axis=1, concat_axis=0, tiled=True
    )


def body(
    enc_state,
    baseline,
    enc_keys,
    dec_queries,
    out_mult,
    doc_lengths,
    expert_ids,
    slot_ids,
    gate_prob,
    norm_gain,
    w_in,
    w_out_t,
    w_value,
):
    enc_len = enc_state.shape[2]
    feature_width = enc_state.shape[3]
    local_experts = w_in.shape[0]
    n_experts = local_experts * lax.axis_size("expert")
    n_dp = lax.axis_size("dp")
    capacity = max(2, 2 * enc_len // n_experts)

    n_peers = lax.axis_size("expert")
    if n_dp == 4 and local_experts == 2 and capacity % 16 == 0 and n_peers & (n_peers - 1) == 0 and feature_width % 512 == 0:
        return whole_pass(
            enc_state[0, 0],
            baseline[0, 0],
            enc_keys[0, 0],
            dec_queries[0, 0],
            out_mult[0, 0],
            doc_lengths,
            expert_ids[0],
            slot_ids[0],
            gate_prob[0],
            norm_gain,
            w_in,
            w_out_t,
            w_value,
            n_peers,
            n_dp,
            capacity,
        )[None, None]

    tokens = enc_state[0, 0].astype(jnp.float32)
    row_scale = norm_gain * lax.rsqrt(jnp.mean(tokens * tokens, axis=-1, keepdims=True) + 1e-06)
    inputs = (tokens * row_scale).astype(jnp.bfloat16)
    base_inputs = (baseline[0, 0].astype(jnp.float32) * row_scale).astype(jnp.bfloat16)
    flat_slot = expert_ids[0, 0] * capacity + slot_ids[0, 0]
    onehot = (
        flat_slot[None, :] == jnp.arange(n_experts * capacity, dtype=jnp.int32)[:, None]
    ).astype(jnp.bfloat16)

    def dispatch(values):
        placed = jnp.dot(onehot, values, preferred_element_type=jnp.float32).astype(jnp.bfloat16)
        return placed.reshape(n_experts, capacity, feature_width)

    layer_mult = attend(
        dec_queries[0, 0], enc_keys[0, 0], out_mult[0, 0], doc_lengths[0, 0], w_value
    )
    scaled_mult = (gate_prob[0, 0][:, None] * layer_mult).astype(jnp.bfloat16)
    sent = (dispatch(inputs), dispatch(base_inputs), dispatch(scaled_mult))
    returned = plain_pass(sent, w_in, w_out_t, n_peers, n_dp)
    per_token = lax.dot_general(
        onehot,
        returned.reshape(n_experts * capacity, feature_width),
        (((0,), (0,)), ((), ())),
        preferred_element_type=jnp.float32,
    )
    result = (layer_mult + row_scale * per_token).astype(jnp.bfloat16)
    return result[None, None]


def solution(mesh):
    in_specs = (
        P("dp", "expert", None, None),
        P("dp", "expert", None, None),
        P("dp", "expert", None, None),
        P("dp", "expert", None, None),
        P("dp", "expert", None, None),
        P("dp", "expert"),
        P("dp", "expert", None),
        P("dp", "expert", None),
        P("dp", "expert", None),
        P(),
        P("expert", None, "dp"),
        P("expert", None, "dp"),
        P(),
    )
    out_specs = P("dp", "expert", None, None)
    return jax.shard_map(body, mesh=mesh, in_specs=in_specs, out_specs=out_specs, check_vma=False)
```
